32 devices in a mesh: fsdp: 32 (over z, y, x, core).
Axes of the slice: x: 2, y: 2, z: 4, core: 2. Of those that a mesh axis runs over, the one named last changes fastest.
Arguments:
- inputs: float32 [2, 32, 256, 384], P(None, 'fsdp'), may hold values from -6 to 6
- cond: float32 [2, 32, 384], P(None, 'fsdp'), may hold values from -6 to 6
- live: int32 [2, 32], P(None, 'fsdp'), may hold values from 0 to 1, as said below
- ada_w: bfloat16 [1, 2304, 384], P(None, 'fsdp'), may hold values from -0.3125 to 0.3125
- attn_w: bfloat16 [1, 1536, 384], P(None, 'fsdp'), may hold values from -0.3125 to 0.3125
- fc1_w: bfloat16 [1, 1536, 384], P(None, 'fsdp'), may hold values from -0.3125 to 0.3125
- fc2_w: bfloat16 [1, 1536, 384], P(None, 'fsdp'), may hold values from -0.15625 to 0.15625
- biases: bfloat16 [1, 5376], P(None, 'fsdp'), may hold values from -3 to 3
- grad_out: float32 [2, 32, 256, 384], P(None, 'fsdp'), may hold values from -6 to 6
Outputs:
- outputs: float32 [2, 32, 256, 384], P(None, 'fsdp')
- d_inputs: float32 [2, 32, 256, 384], P(None, 'fsdp')
- d_cond: float32 [2, 32, 384], P(None, 'fsdp')
- d_ada_w: float32 [1, 2304, 384], P(None, 'fsdp')
- d_attn_w: float32 [1, 1536, 384], P(None, 'fsdp')
- d_fc1_w: float32 [1, 1536, 384], P(None, 'fsdp')
- d_fc2_w: float32 [1, 1536, 384], P(None, 'fsdp')
- d_biases: float32 [1, 5376], P(None, 'fsdp')
The draws below stay inside these ranges and needn't reach their ends.
Inputs may be any that keep to these rules, and one draw needn't show every extreme that they name: `live`: in each micro-batch exactly 17 of the 32 slots hold a latent (1), the others none (0).
All inputs are finite; a program needn't handle non-finite values.
Results may differ from the reference program's by a relative error of at most 0.012.
The reference program's roundings to bfloat16 on the way count: a program that leaves them out, or rounds other values in their place, can miss the bound.
Values may be sent and summed in bfloat16 or wider, within the bound.
No kernel may reach another device: no remote copies, remote signals or barrier semaphores. Data moves between devices by JAX's collectives and lax.ppermute only.
A program may use at most 128 MiB of HBM per device.

```python
import math
import jax
import jax.numpy as jnp
from jax import lax

D = 384
HEADS = 6
FF = 1536
TOK = 256
LAYERS = 1
MB = 2
SLOTS = 32
LIVE = 17
NB = 5376


def draw_cond(key, part):
    base_draw = jnp.clip(jax.random.normal(key, (MB, SLOTS, D), jnp.float32), -6.0, 6.0)
    return base_draw


def draw_live(key, part):
    key_list = jax.random.split(key, MB)
    order_rows = jax.vmap(lambda one_key: jax.random.permutation(one_key, SLOTS))(key_list)
    return (order_rows < LIVE).astype(jnp.int32)


def level_of(stream_key, extent, cuts, smallest, top_value):
    gain = 1.0
    for axis_at, shards_of in cuts:
        steps = jax.random.uniform(jax.random.fold_in(jax.random.fold_in(stream_key, 6), axis_at), (shards_of,), jnp.float32, smallest / len(cuts), top_value / len(cuts))
        gain = gain * jnp.repeat(jnp.exp(steps), extent[axis_at] // shards_of).reshape((-1,) + (1,) * (len(extent) - 1 - axis_at))
    return gain


def centred(stream_key, shape, scale, most, cuts=(), held_as=jnp.bfloat16):
    values = jax.random.normal(stream_key, shape, jnp.float32) * scale
    if len(cuts) > 0:
        values = level_of(stream_key, shape, cuts, -0.22, 0.18) * values
    return jnp.clip(values, min=-most, max=most).astype(held_as)


def setup_inputs(seed: int = 0) -> dict:
    keys = jax.random.split(jax.random.key(seed), 10)
    inputs = centred(keys[0], (MB, SLOTS, TOK, D), 1.0, 6.0, ((1, 32),), jnp.float32)
    cond = draw_cond(jax.random.fold_in(keys[9], 71), 0)
    live = draw_live(jax.random.fold_in(keys[9], 71), 0)
    ada_w = centred(keys[3], (LAYERS, 6 * D, D), D ** -0.5, 0.3125, ((1, 32),))
    attn_w = centred(keys[4], (LAYERS, 4 * D, D), D ** -0.5, 0.3125, ((1, 32),))
    fc1_w = centred(keys[5], (LAYERS, FF, D), D ** -0.5, 0.3125, ((1, 32),))
    fc2_w = centred(keys[6], (LAYERS, FF, D), FF ** -0.5, 0.15625, ((1, 32),))
    biases = centred(keys[7], (LAYERS, NB), 0.5, 3.0, ((1, 32),))
    grad_out = centred(keys[8], (MB, SLOTS, TOK, D), 1.0, 6.0, ((1, 32),), jnp.float32)
    return dict(inputs=inputs, cond=cond, live=live, ada_w=ada_w, attn_w=attn_w, fc1_w=fc1_w, fc2_w=fc2_w, biases=biases, grad_out=grad_out)


NORM_EPS = 1e-06

def product(form, left, right):
    return jnp.einsum(form, left.astype(jnp.float32), right.astype(jnp.float32), precision=lax.Precision.HIGHEST)

def layer_norm(values):
    center = values - lax.optimization_barrier(jnp.mean(values, axis=-1, keepdims=True))
    inv_std = lax.rsqrt(lax.optimization_barrier(jnp.mean(center * center, axis=-1, keepdims=True)) + NORM_EPS)
    return (center * inv_std, inv_std)

def norm_back(grad_norm, normed, inv_std):
    return inv_std * (grad_norm - lax.optimization_barrier(jnp.mean(grad_norm, axis=-1, keepdims=True)) - normed * lax.optimization_barrier(jnp.mean(grad_norm * normed, axis=-1, keepdims=True)))

def gelu_tanh(pre_act):
    return jax.nn.gelu(pre_act, approximate=True)

def forward_layer(layer_in, sc_b, layer_w):
    ada_rows, attn_rows, fc_in, fc_out, bias_row = layer_w
    width_n = layer_in.shape[1]
    hidden = fc_in.shape[0]
    tokens_n = layer_in.shape[0]
    head_dim = width_n // HEADS
    scaling = 1.0 / math.sqrt(head_dim)
    bias_f = bias_row.astype(jnp.float32)
    modulation = product('ed,d->e', ada_rows, sc_b) + bias_f[:6 * width_n]
    shift_a, scale_a, gate_a, shift_b, scale_b, gate_b = jnp.split(modulation, 6)
    normed, inv_std = layer_norm(layer_in)
    h_in = (normed * (1.0 + scale_a) + shift_a).astype(jnp.bfloat16)
    qkv_bias = jnp.concatenate([bias_f[6 * width_n:7 * width_n], jnp.zeros((width_n,), jnp.float32), bias_f[7 * width_n:8 * width_n]])
    qkv_rows = (product('td,ed->te', h_in, attn_rows[:3 * width_n]) + qkv_bias).astype(jnp.bfloat16)
    queries = qkv_rows[:, :width_n].reshape(tokens_n, HEADS, head_dim)
    key_rows = qkv_rows[:, width_n:2 * width_n].reshape(tokens_n, HEADS, head_dim)
    value_rows = qkv_rows[:, 2 * width_n:].reshape(tokens_n, HEADS, head_dim)
    scores = product('thd,shd->hts', queries, key_rows) * scaling
    row_max = lax.optimization_barrier(jnp.max(scores, axis=-1, keepdims=True))
    log_total = row_max + jnp.log(lax.optimization_barrier(jnp.sum(jnp.exp(scores - row_max), axis=-1, keepdims=True)))
    probs_b = jnp.exp(scores - log_total).astype(jnp.bfloat16)
    context = product('hts,shd->thd', probs_b, value_rows).reshape(tokens_n, width_n).astype(jnp.bfloat16)
    attn_out = product('te,de->td', context, attn_rows[3 * width_n:]) + bias_f[8 * width_n:9 * width_n]
    middle = layer_in + gate_a * attn_out
    normed_two, inv_std_two = layer_norm(middle)
    h_mid = (normed_two * (1.0 + scale_b) + shift_b).astype(jnp.bfloat16)
    pre_act = product('td,fd->tf', h_mid, fc_in) + bias_f[9 * width_n:9 * width_n + hidden]
    act_b = gelu_tanh(pre_act).astype(jnp.bfloat16)
    mlp_out = product('tf,fd->td', act_b, fc_out) + bias_f[9 * width_n + hidden:]
    layer_out = middle + gate_b * mlp_out
    kept_acts = (modulation, normed, inv_std, h_in, queries, key_rows, value_rows, log_total, context, attn_out, normed_two, inv_std_two, h_mid, pre_act, act_b, mlp_out)
    return (layer_out, kept_acts)

def backward_layer(grad_y, sc_b, layer_w, kept_acts):
    ada_rows, attn_rows, fc_in, fc_out, bias_row = layer_w
    modulation, normed, inv_std, h_in, queries, key_rows, value_rows, log_total, context, attn_out, normed_two, inv_std_two, h_mid, pre_act, act_b, mlp_out = kept_acts
    width_n = grad_y.shape[1]
    tokens_n = grad_y.shape[0]
    head_dim = width_n // HEADS
    scaling = 1.0 / math.sqrt(head_dim)
    shift_a, scale_a, gate_a, shift_b, scale_b, gate_b = jnp.split(modulation, 6)
    d_gate_b = lax.optimization_barrier(jnp.sum(grad_y * mlp_out, axis=0))
    d_mlp = gate_b * grad_y
    d_mlp_b = d_mlp.astype(jnp.bfloat16)
    g_fc_out = product('tf,td->fd', act_b, d_mlp_b)
    d_act = product('td,fd->tf', d_mlp_b, fc_out)
    d_pre = jax.vjp(gelu_tanh, pre_act)[1](d_act)[0]
    d_pre_b = d_pre.astype(jnp.bfloat16)
    g_fc_in = product('tf,td->fd', d_pre_b, h_mid)
    d_hmid = product('tf,fd->td', d_pre_b, fc_in)
    d_scale_b = lax.optimization_barrier(jnp.sum(d_hmid * normed_two, axis=0))
    d_shift_b = lax.optimization_barrier(jnp.sum(d_hmid, axis=0))
    d_middle = grad_y + norm_back(d_hmid * (1.0 + scale_b), normed_two, inv_std_two)
    d_gate_a = lax.optimization_barrier(jnp.sum(d_middle * attn_out, axis=0))
    d_attn = gate_a * d_middle
    d_attn_b = d_attn.astype(jnp.bfloat16)
    g_out_proj = product('td,te->de', d_attn_b, context)
    d_context = product('td,de->te', d_attn_b, attn_rows[3 * width_n:]).astype(jnp.bfloat16).reshape(tokens_n, HEADS, head_dim)
    scores = product('thd,shd->hts', queries, key_rows) * scaling
    probs_f = jnp.exp(scores - log_total)
    probs_b = probs_f.astype(jnp.bfloat16)
    d_values = product('hts,thd->shd', probs_b, d_context)
    d_probs = product('thd,shd->hts', d_context, value_rows)
    row_dot = lax.optimization_barrier(jnp.sum(probs_f * d_probs, axis=-1, keepdims=True))
    d_scores_b = (probs_f * (d_probs - row_dot)).astype(jnp.bfloat16)
    d_queries = product('hts,shd->thd', d_scores_b, key_rows).reshape(tokens_n, width_n) * scaling
    d_keys = product('hts,thd->shd', d_scores_b, queries).reshape(tokens_n, width_n) * scaling
    d_values = d_values.reshape(tokens_n, width_n)
    d_qkv_b = jnp.concatenate([d_queries, d_keys, d_values], axis=1).astype(jnp.bfloat16)
    g_qkv = product('te,td->ed', d_qkv_b, h_in)
    d_hin = product('te,ed->td', d_qkv_b, attn_rows[:3 * width_n])
    d_scale_a = lax.optimization_barrier(jnp.sum(d_hin * normed, axis=0))
    d_shift_a = lax.optimization_barrier(jnp.sum(d_hin, axis=0))
    d_input = d_middle + norm_back(d_hin * (1.0 + scale_a), normed, inv_std)
    d_mod = jnp.concatenate([d_shift_a, d_scale_a, d_gate_a, d_shift_b, d_scale_b, d_gate_b])
    g_ada = d_mod[:, None] * sc_b.astype(jnp.float32)[None, :]
    d_sc = jnp.dot(d_mod, ada_rows.astype(jnp.float32), precision=lax.Precision.HIGHEST)
    g_bias = jnp.concatenate([d_mod, lax.optimization_barrier(jnp.sum(d_queries, axis=0)), lax.optimization_barrier(jnp.sum(d_values, axis=0)), lax.optimization_barrier(jnp.sum(d_attn, axis=0)), lax.optimization_barrier(jnp.sum(d_pre, axis=0)), lax.optimization_barrier(jnp.sum(d_mlp, axis=0))])
    g_attn = jnp.concatenate([g_qkv, g_out_proj], axis=0)
    return (d_input, d_sc, (g_ada, g_attn, g_fc_in, g_fc_out, g_bias))

def run_latent(layer_in, cond_row, live_flag, grad_row, weights):
    sigmoid_c = jax.nn.sigmoid(cond_row)
    sc_b = (cond_row * sigmoid_c).astype(jnp.bfloat16)
    n_layers = weights[0].shape[0]
    current = layer_in
    kept_all = []
    for layer_idx in range(n_layers):
        layer_w = tuple((stack_w[layer_idx] for stack_w in weights))
        current, kept_acts = forward_layer(current, sc_b, layer_w)
        kept_all.append(kept_acts)
    out_row = live_flag * current
    grad_cur = live_flag * grad_row
    d_sc_sum = jnp.zeros(cond_row.shape, jnp.float32)
    per_layer = [None] * n_layers
    for layer_idx in reversed(range(n_layers)):
        layer_w = tuple((stack_w[layer_idx] for stack_w in weights))
        grad_cur, d_sc, layer_grads = backward_layer(grad_cur, sc_b, layer_w, kept_all[layer_idx])
        d_sc_sum = d_sc_sum + d_sc
        per_layer[layer_idx] = layer_grads
    d_cond_row = d_sc_sum * sigmoid_c * (1.0 + cond_row * (1.0 - sigmoid_c))
    stacked = tuple((jnp.stack([per_layer[layer_idx][member] for layer_idx in range(n_layers)]) for member in range(5)))
    return (out_row, grad_cur, d_cond_row, stacked)

def reference(inputs, cond, live, ada_w, attn_w, fc1_w, fc2_w, biases, grad_out):
    weights = (ada_w, attn_w, fc1_w, fc2_w, biases)
    flat_in = inputs.reshape(MB * SLOTS, TOK, D)
    flat_cond = cond.reshape(MB * SLOTS, D)
    flat_live = live.reshape(MB * SLOTS).astype(jnp.float32)
    flat_grad = grad_out.reshape(MB * SLOTS, TOK, D)
    zero_grads = tuple((jnp.zeros(stack_w.shape, jnp.float32) for stack_w in weights))

    def visit_one(totals, item_row):
        layer_in, cond_row, live_flag, grad_row = item_row
        out_row, d_in, d_cond_row, layer_grads = run_latent(layer_in, cond_row, live_flag, grad_row, weights)
        totals = tuple((total_g + new_g for total_g, new_g in zip(totals, layer_grads)))
        return (totals, (out_row, d_in, d_cond_row))
    totals, (out_rows, d_in_rows, d_cond_rows) = lax.scan(visit_one, zero_grads, (flat_in, flat_cond, flat_live, flat_grad))
    return (out_rows.reshape(MB, SLOTS, TOK, D), d_in_rows.reshape(MB, SLOTS, TOK, D), d_cond_rows.reshape(MB, SLOTS, D), totals[0], totals[1], totals[2], totals[3], totals[4])
```

```python
import math

import jax
import jax.numpy as jnp
from jax import lax
from jax.sharding import PartitionSpec as P

HEADS = 6


NORM_EPS = 1e-06


def product(form, left, right):
    return jnp.einsum(form, left, right, preferred_element_type=jnp.float32)


def layer_norm(values):
    center = values - jnp.mean(values, axis=-1, keepdims=True)
    inv_std = lax.rsqrt(jnp.mean(center * center, axis=-1, keepdims=True) + NORM_EPS)
    return (center * inv_std, inv_std)


def norm_back(grad_norm, normed, inv_std):
    return inv_std * (
        grad_norm
        - jnp.mean(grad_norm, axis=-1, keepdims=True)
        - normed * jnp.mean(grad_norm * normed, axis=-1, keepdims=True)
    )


def gelu_tanh(pre_act):
    return jax.nn.gelu(pre_act, approximate=True)


def forward_layer(layer_in, sc_b, layer_w):
    ada_rows, attn_rows, fc_in, fc_out, bias_row = layer_w
    width_n = layer_in.shape[1]
    hidden = fc_in.shape[0]
    tokens_n = layer_in.shape[0]
    head_dim = width_n // HEADS
    scaling = 1.0 / math.sqrt(head_dim)
    bias_f = bias_row.astype(jnp.float32)
    modulation = product("ed,d->e", ada_rows, sc_b) + bias_f[: 6 * width_n]
    shift_a, scale_a, gate_a, shift_b, scale_b, gate_b = jnp.split(modulation, 6)
    normed, inv_std = layer_norm(layer_in)
    h_in = (normed * (1.0 + scale_a) + shift_a).astype(jnp.bfloat16)
    qkv_bias = jnp.concatenate(
        [
            bias_f[6 * width_n : 7 * width_n],
            jnp.zeros((width_n,), jnp.float32),
            bias_f[7 * width_n : 8 * width_n],
        ]
    )
    qkv_rows = (product("td,ed->te", h_in, attn_rows[: 3 * width_n]) + qkv_bias).astype(
        jnp.bfloat16
    )
    queries = qkv_rows[:, :width_n].reshape(tokens_n, HEADS, head_dim)
    key_rows = qkv_rows[:, width_n : 2 * width_n].reshape(tokens_n, HEADS, head_dim)
    value_rows = qkv_rows[:, 2 * width_n :].reshape(tokens_n, HEADS, head_dim)
    scores = product("thd,shd->hts", queries, key_rows) * scaling
    row_max = jnp.max(scores, axis=-1, keepdims=True)
    log_total = row_max + jnp.log(jnp.sum(jnp.exp(scores - row_max), axis=-1, keepdims=True))
    probs_b = jnp.exp(scores - log_total).astype(jnp.bfloat16)
    context = (
        product("hts,shd->thd", probs_b, value_rows).reshape(tokens_n, width_n).astype(jnp.bfloat16)
    )
    attn_out = (
        product("te,de->td", context, attn_rows[3 * width_n :]) + bias_f[8 * width_n : 9 * width_n]
    )
    middle = layer_in + gate_a * attn_out
    normed_two, inv_std_two = layer_norm(middle)
    h_mid = (normed_two * (1.0 + scale_b) + shift_b).astype(jnp.bfloat16)
    pre_act = product("td,fd->tf", h_mid, fc_in) + bias_f[9 * width_n : 9 * width_n + hidden]
    act_b = gelu_tanh(pre_act).astype(jnp.bfloat16)
    mlp_out = product("tf,fd->td", act_b, fc_out) + bias_f[9 * width_n + hidden :]
    layer_out = middle + gate_b * mlp_out
    kept_acts = (
        modulation,
        normed,
        inv_std,
        h_in,
        queries,
        key_rows,
        value_rows,
        log_total,
        context,
        attn_out,
        normed_two,
        inv_std_two,
        h_mid,
        pre_act,
        act_b,
        mlp_out,
    )
    return (layer_out, kept_acts)


def backward_layer(grad_y, sc_b, layer_w, kept_acts):
    ada_rows, attn_rows, fc_in, fc_out, bias_row = layer_w
    (
        modulation,
        normed,
        inv_std,
        h_in,
        queries,
        key_rows,
        value_rows,
        log_total,
        context,
        attn_out,
        normed_two,
        inv_std_two,
        h_mid,
        pre_act,
        act_b,
        mlp_out,
    ) = kept_acts
    width_n = grad_y.shape[1]
    tokens_n = grad_y.shape[0]
    head_dim = width_n // HEADS
    scaling = 1.0 / math.sqrt(head_dim)
    shift_a, scale_a, gate_a, shift_b, scale_b, gate_b = jnp.split(modulation, 6)
    d_gate_b = jnp.sum(grad_y * mlp_out, axis=0)
    d_mlp = gate_b * grad_y
    d_mlp_b = d_mlp.astype(jnp.bfloat16)
    g_fc_out = product("tf,td->fd", act_b, d_mlp_b)
    d_act = product("td,fd->tf", d_mlp_b, fc_out)
    d_pre = jax.vjp(gelu_tanh, pre_act)[1](d_act)[0]
    d_pre_b = d_pre.astype(jnp.bfloat16)
    g_fc_in = product("tf,td->fd", d_pre_b, h_mid)
    d_hmid = product("tf,fd->td", d_pre_b, fc_in)
    d_scale_b = jnp.sum(d_hmid * normed_two, axis=0)
    d_shift_b = jnp.sum(d_hmid, axis=0)
    d_middle = grad_y + norm_back(d_hmid * (1.0 + scale_b), normed_two, inv_std_two)
    d_gate_a = jnp.sum(d_middle * attn_out, axis=0)
    d_attn = gate_a * d_middle
    d_attn_b = d_attn.astype(jnp.bfloat16)
    g_out_proj = product("td,te->de", d_attn_b, context)
    d_context = (
        product("td,de->te", d_attn_b, attn_rows[3 * width_n :])
        .astype(jnp.bfloat16)
        .reshape(tokens_n, HEADS, head_dim)
    )
    scores = product("thd,shd->hts", queries, key_rows) * scaling
    probs_f = jnp.exp(scores - log_total)
    probs_b = probs_f.astype(jnp.bfloat16)
    d_values = product("hts,thd->shd", probs_b, d_context)
    d_probs = product("thd,shd->hts", d_context, value_rows)
    row_dot = jnp.sum(probs_f * d_probs, axis=-1, keepdims=True)
    d_scores_b = (probs_f * (d_probs - row_dot)).astype(jnp.bfloat16)
    d_queries = product("hts,shd->thd", d_scores_b, key_rows).reshape(tokens_n, width_n) * scaling
    d_keys = product("hts,thd->shd", d_scores_b, queries).reshape(tokens_n, width_n) * scaling
    d_values = d_values.reshape(tokens_n, width_n)
    d_qkv_b = jnp.concatenate([d_queries, d_keys, d_values], axis=1).astype(jnp.bfloat16)
    g_qkv = product("te,td->ed", d_qkv_b, h_in)
    d_hin = product("te,ed->td", d_qkv_b, attn_rows[: 3 * width_n])
    d_scale_a = jnp.sum(d_hin * normed, axis=0)
    d_shift_a = jnp.sum(d_hin, axis=0)
    d_input = d_middle + norm_back(d_hin * (1.0 + scale_a), normed, inv_std)
    d_mod = jnp.concatenate([d_shift_a, d_scale_a, d_gate_a, d_shift_b, d_scale_b, d_gate_b])
    g_ada = d_mod[:, None] * sc_b.astype(jnp.float32)[None, :]
    d_sc = jnp.dot(d_mod, ada_rows.astype(jnp.float32), precision=lax.Precision.HIGHEST)
    g_bias = jnp.concatenate(
        [
            d_mod,
            jnp.sum(d_queries, axis=0),
            jnp.sum(d_values, axis=0),
            jnp.sum(d_attn, axis=0),
            jnp.sum(d_pre, axis=0),
            jnp.sum(d_mlp, axis=0),
        ]
    )
    g_attn = jnp.concatenate([g_qkv, g_out_proj], axis=0)
    return (d_input, d_sc, d_mod, (g_ada, g_attn, g_fc_in, g_fc_out, g_bias))


def run_forward(layer_in, cond_row, weights):
    sc_b = (cond_row * jax.nn.sigmoid(cond_row)).astype(jnp.bfloat16)
    current = layer_in
    layer_w = tuple((stack_w[0] for stack_w in weights))
    current, kept_acts = forward_layer(current, sc_b, layer_w)
    kept_all = [kept_acts]
    return (current, sc_b, kept_all)


def run_backward(grad_row, cond_row, sc_b, kept_all, weights):
    n_layers = weights[0].shape[0]
    grad_cur = grad_row
    d_sc_sum = jnp.zeros(cond_row.shape, jnp.float32)
    per_layer = [None] * n_layers
    mod_rows = [None] * n_layers
    for layer_idx in reversed(range(n_layers)):
        layer_w = tuple((stack_w[layer_idx] for stack_w in weights))
        grad_cur, d_sc, d_mod, layer_grads = backward_layer(
            grad_cur, sc_b, layer_w, kept_all[layer_idx]
        )
        d_sc_sum = d_sc
        per_layer[layer_idx] = layer_grads
        mod_rows[layer_idx] = d_mod
    sigmoid_c = jax.nn.sigmoid(cond_row)
    d_cond_row = d_sc_sum * sigmoid_c * (1.0 + cond_row * (1.0 - sigmoid_c))
    return (grad_cur, d_cond_row, per_layer, jnp.stack(mod_rows))


def gather_orders(count):
    high = list(range(count - 1, 2, -1))
    near = [k for k in (2, 1) if k < count]
    return high + near + [0], high + near[::-1] + [0]


def exchange(value, bit_idx, group_n):
    return lax.ppermute(value, "fsdp", [(dev, dev ^ (1 << bit_idx)) for dev in range(group_n)])


def own_bit(bit_idx):
    return (lax.axis_index("fsdp") >> bit_idx) & 1


def gather_blocks(block, order):
    count = len(order)
    cur = block.reshape((1,) * count + block.shape)
    for bit_idx in order:
        other = exchange(cur, bit_idx, 1 << count)
        upper = own_bit(bit_idx) == 1
        cur = jnp.concatenate(
            [jnp.where(upper, other, cur), jnp.where(upper, cur, other)], axis=count - 1 - bit_idx
        )
    return cur


def scatter_sum(blocks, order):
    count = len(order)
    cur = blocks
    for step, bit_idx in enumerate(order):
        axis = count - 1 - bit_idx
        mine = own_bit(bit_idx)
        other = exchange(
            lax.dynamic_index_in_dim(cur, 1 - mine, axis, keepdims=True), bit_idx, 1 << count
        )
        kept = lax.dynamic_index_in_dim(cur, mine, axis, keepdims=True)
        total = kept.astype(jnp.float32) + other.astype(jnp.float32)
        cur = total if step == count - 1 else total.astype(jnp.bfloat16)
    return cur.reshape(blocks.shape[count:])


def swap_blocks(blocks, order):
    count = len(order)
    cur = blocks
    for bit_idx in order:
        axis = count - 1 - bit_idx
        mine = own_bit(bit_idx)
        other = exchange(
            lax.dynamic_index_in_dim(cur, 1 - mine, axis, keepdims=True), bit_idx, 1 << count
        )
        kept = lax.dynamic_index_in_dim(cur, mine, axis, keepdims=True)
        upper = mine == 1
        cur = jnp.concatenate(
            [jnp.where(upper, other, kept), jnp.where(upper, kept, other)], axis=axis
        )
    return cur


def local(inputs, cond, live, ada_w, attn_w, fc1_w, fc2_w, biases, grad_out):
    group_n = lax.axis_size("fsdp")
    count = group_n.bit_length() - 1
    first, second = gather_orders(count)
    width_n = attn_w.shape[2]
    batches = inputs.shape[0]
    own_ada, own_bias = ada_w.shape[1], biases.shape[1]
    sc_own = (cond[:, 0] * jax.nn.sigmoid(cond[:, 0])).astype(jnp.bfloat16)
    bias_line = jnp.pad(biases, ((0, 0), (0, width_n - own_bias)))
    side_rows = own_ada + 1 + batches
    pad_rows = -side_rows % 16
    side = jnp.concatenate(
        [ada_w[0], bias_line, sc_own, jnp.zeros((pad_rows, width_n), jnp.bfloat16)], axis=0
    )
    side_all = gather_blocks(side, second).reshape(group_n, side_rows + pad_rows, width_n)
    attn_all = gather_blocks(attn_w[0], first).reshape(1, -1, width_n)
    fc1_all = gather_blocks(fc1_w[0], first).reshape(1, -1, width_n)
    fc2_all = gather_blocks(fc2_w[0], second).reshape(1, -1, width_n)
    ada_all = side_all[:, :own_ada].reshape(1, -1, width_n)
    bias_all = side_all[:, own_ada, :own_bias].reshape(1, -1)
    sc_all = side_all[:, own_ada + 1 : own_ada + 1 + batches]
    weights = (ada_all, attn_all, fc1_all, fc2_all, bias_all)
    totals = [0.0] * 5
    out_rows, d_in_rows, d_cond_rows, mod_list = ([], [], [], [])
    for batch_idx in range(batches):
        live_flag = live[batch_idx, 0].astype(jnp.float32)
        last_out, sc_b, kept_all = run_forward(inputs[batch_idx, 0], cond[batch_idx, 0], weights)
        d_in, d_cond_row, per_layer, mod_stack = run_backward(
            live_flag * grad_out[batch_idx, 0], cond[batch_idx, 0], sc_b, kept_all, weights
        )
        for member in range(1, 5):
            totals[member] = totals[member] + per_layer[0][member]
        mod_list.append(mod_stack[0])
        out_rows.append((live_flag * last_out)[None])
        d_in_rows.append(d_in[None])
        d_cond_rows.append(d_cond_row[None])
    cube = (2,) * count
    sums = [
        scatter_sum(totals[member].astype(jnp.bfloat16).reshape(cube + (-1, width_n)), order[::-1])
        for member, order in ((1, first), (2, first), (3, second))
    ]
    mods = jnp.stack(mod_list).reshape(batches, group_n, own_ada)
    side_grads = jnp.concatenate(
        [mods[idx] for idx in range(batches)] + [totals[4].reshape(group_n, own_bias)], axis=1
    )
    swapped = swap_blocks(side_grads.reshape(cube + (1, -1)), second[::-1]).reshape(group_n, -1)
    own_mods = swapped[:, : batches * own_ada].reshape(group_n * batches, own_ada)
    d_bias = jnp.sum(swapped[:, batches * own_ada :], axis=0)
    d_ada = jnp.einsum(
        "kr,kd->rd",
        own_mods,
        sc_all.reshape(group_n * batches, width_n).astype(jnp.float32),
        precision=lax.Precision.HIGHEST,
    )
    return (
        jnp.stack(out_rows),
        jnp.stack(d_in_rows),
        jnp.stack(d_cond_rows),
        d_ada[None],
        sums[0][None],
        sums[1][None],
        sums[2][None],
        d_bias[None],
    )


def solution(mesh):
    return jax.shard_map(
        local,
        mesh=mesh,
        in_specs=(
            P(None, "fsdp", None, None),
            P(None, "fsdp", None),
            P(None, "fsdp"),
            P(None, "fsdp", None),
            P(None, "fsdp", None),
            P(None, "fsdp", None),
            P(None, "fsdp", None),
            P(None, "fsdp"),
            P(None, "fsdp", None, None),
        ),
        out_specs=(
            P(None, "fsdp", None, None),
            P(None, "fsdp", None, None),
            P(None, "fsdp", None),
            P(None, "fsdp", None),
            P(None, "fsdp", None),
            P(None, "fsdp", None),
            P(None, "fsdp", None),
            P(None, "fsdp"),
        ),
        check_vma=False,
    )
```

```python
import functools
import math

import jax
import jax.numpy as jnp
from jax import lax
from jax.experimental import pallas as pl
from jax.experimental.pallas import tpu as pltpu
from jax.sharding import PartitionSpec as P

HEADS = 6

CHUNK = 512

NORM_EPS = 1e-06


def product(form, left, right):
    return jnp.einsum(form, left, right, preferred_element_type=jnp.float32)


def dot_nn(left, right):
    return lax.dot_general(left, right, (((1,), (0,)), ((), ())), preferred_element_type=jnp.float32)


def dot_nt(left, right):
    return lax.dot_general(left, right, (((1,), (1,)), ((), ())), preferred_element_type=jnp.float32)


def dot_tn(left, right):
    return lax.dot_general(left, right, (((0,), (0,)), ((), ())), preferred_element_type=jnp.float32)


def layer_norm(values):
    center = values - jnp.mean(values, axis=-1, keepdims=True)
    inv_std = lax.rsqrt(jnp.mean(center * center, axis=-1, keepdims=True) + NORM_EPS)
    return (center * inv_std, inv_std)


def norm_back(grad_norm, normed, inv_std):
    return inv_std * (
        grad_norm
        - jnp.mean(grad_norm, axis=-1, keepdims=True)
        - normed * jnp.mean(grad_norm * normed, axis=-1, keepdims=True)
    )


def token_sum(values):
    return jnp.sum(values, axis=0, keepdims=True)


def pair_masks(rows, pair_w):
    lane = lax.broadcasted_iota(jnp.int32, (rows, pair_w), 1)
    return (lane < pair_w // 2, lane >= pair_w // 2)


def attend_kernel(batches, x_ref, mod_ref, w_ref, bias_ref, h_ref, qkv_ref, p_ref, ctx_ref, ao_ref, mid_ref):
    tokens_n, width_n = x_ref.shape[0] // batches, x_ref.shape[1]
    pair_w = 2 * (width_n // HEADS)
    scaling = 1.0 / math.sqrt(width_n // HEADS)
    for b in range(batches):
        rows = pl.ds(b * tokens_n, tokens_n)
        normed, _ = layer_norm(x_ref[rows, :])
        shift = mod_ref[b, 0:1, :]
        scale = mod_ref[b, 1:2, :]
        h_ref[rows, :] = (normed * (1.0 + scale) + shift).astype(jnp.bfloat16)
    for part, bias_row in ((0, 6), (1, None), (2, 7)):
        cols = pl.ds(part * width_n, width_n)
        value = dot_nt(h_ref[...], w_ref[cols, :])
        if bias_row is not None:
            value = value + bias_ref[bias_row : bias_row + 1, :]
        qkv_ref[:, cols] = value.astype(jnp.bfloat16)
    masks = pair_masks(tokens_n, pair_w)
    for b in range(batches):
        rows = pl.ds(b * tokens_n, tokens_n)
        for pair in range(HEADS // 2):
            q_pair = qkv_ref[rows, pl.ds(pair * pair_w, pair_w)]
            k_pair = qkv_ref[rows, pl.ds(width_n + pair * pair_w, pair_w)]
            v_pair = qkv_ref[rows, pl.ds(2 * width_n + pair * pair_w, pair_w)]
            found = []
            for side in range(2):
                q_one = jnp.where(masks[side], q_pair, jnp.zeros_like(q_pair)) * jnp.bfloat16(scaling)
                scores = dot_nt(q_one, k_pair)
                expd = jnp.exp(scores - jnp.max(scores, axis=-1, keepdims=True))
                share = 1.0 / jnp.sum(expd, axis=-1, keepdims=True)
                probs = (expd * share).astype(jnp.bfloat16)
                p_ref[b * HEADS + 2 * pair + side] = probs
                found.append(dot_nn(probs, v_pair))
            ctx_ref[rows, pl.ds(pair * pair_w, pair_w)] = jnp.where(masks[0], *found).astype(jnp.bfloat16)
    attn_out = dot_nt(ctx_ref[...], w_ref[pl.ds(3 * width_n, width_n), :]) + bias_ref[8:9, :]
    ao_ref[...] = attn_out
    for b in range(batches):
        rows = pl.ds(b * tokens_n, tokens_n)
        mid_ref[rows, :] = x_ref[rows, :] + mod_ref[b, 2:3, :] * ao_ref[rows, :]


def mlp_kernel(
    batches, live_ref, mid_ref, grad_ref, mod_ref, bias_ref, b_in_ref, w_in_ref, w_out_ref,
    out_ref, dmid_ref, g_in_ref, g_out_ref, gb_in_ref, gb_out_ref, dmod_ref,
    h_ref, dmlp_ref, mlp_ref, dh_ref,
):
    step = pl.program_id(0)
    tokens_n, width_n = mid_ref.shape[0] // batches, mid_ref.shape[1]

    @pl.when(step == 0)
    def _():
        total = jnp.zeros((1, width_n), jnp.float32)
        for b in range(batches):
            rows = pl.ds(b * tokens_n, tokens_n)
            normed, _ = layer_norm(mid_ref[rows, :])
            h_ref[rows, :] = (normed * (1.0 + mod_ref[b, 4:5, :]) + mod_ref[b, 3:4, :]).astype(jnp.bfloat16)
            d_mlp = mod_ref[b, 5:6, :] * (live_ref[b].astype(jnp.float32) * grad_ref[rows, :])
            total = total + token_sum(d_mlp)
            dmlp_ref[rows, :] = d_mlp.astype(jnp.bfloat16)
        gb_out_ref[...] = total
        mlp_ref[...] = jnp.zeros_like(mlp_ref)
        dh_ref[...] = jnp.zeros_like(dh_ref)

    pre = dot_nt(h_ref[...], w_in_ref[...]) + b_in_ref[...]
    root = math.sqrt(2.0 / math.pi)
    square = pre * pre
    tanh = jnp.tanh(root * (pre + 0.044715 * (square * pre)))
    half = 0.5 * (1.0 + tanh)
    act = (pre * half).astype(jnp.bfloat16)
    slope = half + (0.5 * pre) * (1.0 - tanh * tanh) * (root + (3.0 * 0.044715 * root) * square)
    d_pre = dot_nt(dmlp_ref[...], w_out_ref[...]) * slope
    mlp_ref[...] += dot_nn(act, w_out_ref[...])
    g_out_ref[...] = dot_tn(act, dmlp_ref[...]).astype(jnp.bfloat16)
    gb_in_ref[...] = token_sum(d_pre)
    d_pre_b = d_pre.astype(jnp.bfloat16)
    dh_ref[...] += dot_nn(d_pre_b, w_in_ref[...])
    g_in_ref[...] = dot_tn(d_pre_b, h_ref[...]).astype(jnp.bfloat16)

    @pl.when(step == pl.num_programs(0) - 1)
    def _():
        for b in range(batches):
            rows = pl.ds(b * tokens_n, tokens_n)
            live = live_ref[b].astype(jnp.float32)
            middle = mid_ref[rows, :]
            d_y = live * grad_ref[rows, :]
            mlp_out = mlp_ref[rows, :] + bias_ref[13:14, :]
            out_ref[rows, :] = live * (middle + mod_ref[b, 5:6, :] * mlp_out)
            normed, inv_std = layer_norm(middle)
            d_h = dh_ref[rows, :]
            dmod_ref[b, 0:1, :] = token_sum(d_h)
            dmod_ref[b, 1:2, :] = token_sum(d_h * normed)
            dmod_ref[b, 2:3, :] = token_sum(d_y * mlp_out)
            dmid_ref[rows, :] = d_y + norm_back(d_h * (1.0 + mod_ref[b, 4:5, :]), normed, inv_std)


def attend_back_kernel(
    batches, x_ref, mod_ref, w_ref, h_ref, qkv_ref, p_ref, ctx_ref, ao_ref, dmid_ref,
    dx_ref, g_ref, gb_ref, dmod_ref, dattn_ref, dctx_ref, dqkv_ref,
):
    tokens_n, width_n = x_ref.shape[0] // batches, x_ref.shape[1]
    pair_w = 2 * (width_n // HEADS)
    scaling = 1.0 / math.sqrt(width_n // HEADS)
    total = jnp.zeros((1, width_n), jnp.float32)
    for b in range(batches):
        rows = pl.ds(b * tokens_n, tokens_n)
        d_mid = dmid_ref[rows, :]
        dmod_ref[b, 2:3, :] = token_sum(d_mid * ao_ref[rows, :])
        d_attn = mod_ref[b, 2:3, :] * d_mid
        total = total + token_sum(d_attn)
        dattn_ref[rows, :] = d_attn.astype(jnp.bfloat16)
    gb_ref[2:3, :] = total
    dctx_ref[...] = dot_nn(dattn_ref[...], w_ref[pl.ds(3 * width_n, width_n), :]).astype(jnp.bfloat16)
    g_ref[pl.ds(3 * width_n, width_n), :] = dot_tn(dattn_ref[...], ctx_ref[...]).astype(jnp.bfloat16)
    masks = pair_masks(tokens_n, pair_w)
    for pair in range(HEADS // 2):
        cols = pl.ds(pair * pair_w, pair_w)
        q_total = jnp.zeros((1, pair_w), jnp.float32)
        v_total = jnp.zeros((1, pair_w), jnp.float32)
        for b in range(batches):
            rows = pl.ds(b * tokens_n, tokens_n)
            q_pair = qkv_ref[rows, cols]
            k_pair = qkv_ref[rows, pl.ds(width_n + pair * pair_w, pair_w)]
            v_pair = qkv_ref[rows, pl.ds(2 * width_n + pair * pair_w, pair_w)]
            dc_pair = dctx_ref[rows, cols]
            d_q, d_k, d_v = [], [], []
            for side in range(2):
                probs_b = p_ref[b * HEADS + 2 * pair + side]
                probs = probs_b.astype(jnp.float32)
                dc_one = jnp.where(masks[side], dc_pair, jnp.zeros_like(dc_pair))
                d_probs = dot_nt(dc_one, v_pair)
                row_dot = jnp.sum(probs * d_probs, axis=-1, keepdims=True)
                d_scores = (probs * (d_probs - row_dot)).astype(jnp.bfloat16)
                d_v.append(dot_tn(probs_b, dc_pair))
                d_q.append(dot_nn(d_scores, k_pair))
                d_k.append(dot_tn(d_scores, q_pair))
            d_query = jnp.where(masks[0], *d_q) * scaling
            d_key = jnp.where(masks[0], *d_k) * scaling
            d_value = jnp.where(masks[0], *d_v)
            q_total = q_total + token_sum(d_query)
            v_total = v_total + token_sum(d_value)
            dqkv_ref[rows, cols] = d_query.astype(jnp.bfloat16)
            dqkv_ref[rows, pl.ds(width_n + pair * pair_w, pair_w)] = d_key.astype(jnp.bfloat16)
            dqkv_ref[rows, pl.ds(2 * width_n + pair * pair_w, pair_w)] = d_value.astype(jnp.bfloat16)
        gb_ref[0:1, cols] = q_total
        gb_ref[1:2, cols] = v_total
    for part in range(3):
        cols = pl.ds(part * width_n, width_n)
        g_ref[cols, :] = dot_tn(dqkv_ref[:, cols], h_ref[...]).astype(jnp.bfloat16)
    d_h_all = dot_nn(dqkv_ref[...], w_ref[pl.ds(0, 3 * width_n), :])
    for b in range(batches):
        rows = pl.ds(b * tokens_n, tokens_n)
        normed, inv_std = layer_norm(x_ref[rows, :])
        d_h = d_h_all[b * tokens_n : (b + 1) * tokens_n]
        dmod_ref[b, 0:1, :] = token_sum(d_h)
        dmod_ref[b, 1:2, :] = token_sum(d_h * normed)
        dx_ref[rows, :] = dmid_ref[rows, :] + norm_back(d_h * (1.0 + mod_ref[b, 1:2, :]), normed, inv_std)


def shaped(shape, dtype):
    return jax.ShapeDtypeStruct(shape, dtype)


def attend(x_rows, mods, weight, bias_rows):
    batches = mods.shape[0]
    total_n, width_n = x_rows.shape
    tokens_n = total_n // batches
    return pl.pallas_call(
        functools.partial(attend_kernel, batches),
        out_shape=(
            shaped((total_n, width_n), jnp.bfloat16),
            shaped((total_n, 3 * width_n), jnp.bfloat16),
            shaped((batches * HEADS, tokens_n, tokens_n), jnp.bfloat16),
            shaped((total_n, width_n), jnp.bfloat16),
            shaped((total_n, width_n), jnp.float32),
            shaped((total_n, width_n), jnp.float32),
        ),
        name="attend",
    )(x_rows, mods, weight, bias_rows)


def mlp(live_flags, middle, grad_rows, mods, bias_rows, bias_in, w_in, w_out):
    batches = mods.shape[0]
    total_n, width_n = middle.shape
    hidden = w_in.shape[0]
    chunk = CHUNK
    whole = lambda *shape: pl.BlockSpec(shape, lambda i: (0,) * len(shape))
    part = pl.BlockSpec((chunk, width_n), lambda i: (i, 0))
    line = pl.BlockSpec((1, chunk), lambda i: (0, i))
    return pl.pallas_call(
        functools.partial(mlp_kernel, batches),
        grid=(hidden // chunk,),
        in_specs=[
            pl.BlockSpec(memory_space=pltpu.SMEM),
            whole(total_n, width_n),
            whole(total_n, width_n),
            whole(*mods.shape),
            whole(*bias_rows.shape),
            line,
            part,
            part,
        ],
        out_specs=(
            whole(total_n, width_n),
            whole(total_n, width_n),
            part,
            part,
            line,
            whole(1, width_n),
            whole(batches, 3, width_n),
        ),
        out_shape=(
            shaped((total_n, width_n), jnp.float32),
            shaped((total_n, width_n), jnp.float32),
            shaped((hidden, width_n), jnp.bfloat16),
            shaped((hidden, width_n), jnp.bfloat16),
            shaped((1, hidden), jnp.float32),
            shaped((1, width_n), jnp.float32),
            shaped((batches, 3, width_n), jnp.float32),
        ),
        scratch_shapes=[
            pltpu.VMEM((total_n, width_n), jnp.bfloat16),
            pltpu.VMEM((total_n, width_n), jnp.bfloat16),
            pltpu.VMEM((total_n, width_n), jnp.float32),
            pltpu.VMEM((total_n, width_n), jnp.float32),
        ],
        name="mlp",
    )(live_flags, middle, grad_rows, mods, bias_rows, bias_in, w_in, w_out)


def attend_back(x_rows, mods, weight, kept, d_mid):
    batches = mods.shape[0]
    total_n, width_n = x_rows.shape
    return pl.pallas_call(
        functools.partial(attend_back_kernel, batches),
        out_shape=(
            shaped((total_n, width_n), jnp.float32),
            shaped((4 * width_n, width_n), jnp.bfloat16),
            shaped((3, width_n), jnp.float32),
            shaped((batches, 3, width_n), jnp.float32),
        ),
        scratch_shapes=[
            pltpu.VMEM((total_n, width_n), jnp.bfloat16),
            pltpu.VMEM((total_n, width_n), jnp.bfloat16),
            pltpu.VMEM((total_n, 3 * width_n), jnp.bfloat16),
        ],
        name="attend_back",
    )(x_rows, mods, weight, *kept, d_mid)


def gather_orders(count):
    high = list(range(count - 1, 2, -1))
    near = [k for k in (2, 1) if k < count]
    return high + near + [0], high + near[::-1] + [0]


def exchange(value, bit_idx, group_n):
    return lax.ppermute(value, "fsdp", [(dev, dev ^ (1 << bit_idx)) for dev in range(group_n)])


def own_bit(bit_idx):
    return (lax.axis_index("fsdp") >> bit_idx) & 1


def gather_blocks(block, order):
    count = len(order)
    cur = block.reshape((1,) * count + block.shape)
    for bit_idx in order:
        other = exchange(cur, bit_idx, 1 << count)
        upper = own_bit(bit_idx) == 1
        cur = jnp.concatenate(
            [jnp.where(upper, other, cur), jnp.where(upper, cur, other)], axis=count - 1 - bit_idx
        )
    return cur


def scatter_sum(blocks, order):
    count = len(order)
    cur = blocks
    for step, bit_idx in enumerate(order):
        axis = count - 1 - bit_idx
        mine = own_bit(bit_idx)
        other = exchange(
            lax.dynamic_index_in_dim(cur, 1 - mine, axis, keepdims=True), bit_idx, 1 << count
        )
        kept = lax.dynamic_index_in_dim(cur, mine, axis, keepdims=True)
        total = kept.astype(jnp.float32) + other.astype(jnp.float32)
        cur = total if step == count - 1 else total.astype(jnp.bfloat16)
    return cur.reshape(blocks.shape[count:])


def swap_blocks(blocks, order):
    count = len(order)
    cur = blocks
    for bit_idx in order:
        axis = count - 1 - bit_idx
        mine = own_bit(bit_idx)
        other = exchange(
            lax.dynamic_index_in_dim(cur, 1 - mine, axis, keepdims=True), bit_idx, 1 << count
        )
        kept = lax.dynamic_index_in_dim(cur, mine, axis, keepdims=True)
        upper = mine == 1
        cur = jnp.concatenate(
            [jnp.where(upper, other, kept), jnp.where(upper, kept, other)], axis=axis
        )
    return cur


def local(inputs, cond, live, ada_w, attn_w, fc1_w, fc2_w, biases, grad_out):
    group_n = lax.axis_size("fsdp")
    count = group_n.bit_length() - 1
    first, second = gather_orders(count)
    width_n = attn_w.shape[2]
    batches = inputs.shape[0]
    own_ada, own_bias = ada_w.shape[1], biases.shape[1]
    cond_rows = cond[:, 0]
    sigmoid_c = jax.nn.sigmoid(cond_rows)
    sc_own = (cond_rows * sigmoid_c).astype(jnp.bfloat16)
    bias_line = jnp.pad(biases, ((0, 0), (0, width_n - own_bias)))
    side_rows = own_ada + 1 + batches
    pad_rows = -side_rows % 16
    side = jnp.concatenate(
        [ada_w[0], bias_line, sc_own, jnp.zeros((pad_rows, width_n), jnp.bfloat16)], axis=0
    )
    side_all = gather_blocks(side, second).reshape(group_n, side_rows + pad_rows, width_n)
    attn_all = gather_blocks(attn_w[0], first).reshape(-1, width_n)
    fc1_all = gather_blocks(fc1_w[0], first).reshape(-1, width_n)
    fc2_all = gather_blocks(fc2_w[0], second).reshape(-1, width_n)
    ada_all = side_all[:, :own_ada].reshape(-1, width_n)
    bias_rows = side_all[:, own_ada, :own_bias].reshape(-1, width_n).astype(jnp.float32)
    sc_all = side_all[:, own_ada + 1 : own_ada + 1 + batches]
    hidden = fc1_all.shape[0]
    mods = product("ed,bd->be", ada_all, sc_own).reshape(batches, 6, width_n) + bias_rows[:6]
    x_rows = inputs.reshape(-1, width_n)
    h_in, qkv, probs, context, attn_out, middle = attend(x_rows, mods, attn_all, bias_rows)
    out, d_mid, g_fc1, g_fc2, gb_in, gb_out, dmod_b = mlp(
        live[:, 0],
        middle,
        grad_out.reshape(-1, width_n),
        mods,
        bias_rows,
        bias_rows[9:13].reshape(1, hidden),
        fc1_all,
        fc2_all,
    )
    d_x, g_attn, gb_attn, dmod_a = attend_back(
        x_rows, mods, attn_all, (h_in, qkv, probs, context, attn_out), d_mid
    )
    d_mods = jnp.concatenate([dmod_a, dmod_b], axis=1)
    d_sc = jnp.einsum(
        "be,ed->bd",
        d_mods.reshape(batches, -1),
        ada_all.astype(jnp.float32),
        precision=lax.Precision.HIGHEST,
    )
    d_cond = d_sc * sigmoid_c * (1.0 + cond_rows * (1.0 - sigmoid_c))
    g_bias = jnp.concatenate(
        [jnp.sum(d_mods, axis=0), gb_attn, gb_in.reshape(-1, width_n), gb_out], axis=0
    )
    cube = (2,) * count
    sums = [
        scatter_sum(value.reshape(cube + (-1, width_n)), order[::-1])
        for value, order in ((g_attn, first), (g_fc1, first), (g_fc2, second))
    ]
    mod_blocks = d_mods.reshape(batches, group_n, own_ada)
    side_grads = jnp.concatenate(
        [mod_blocks[idx] for idx in range(batches)] + [g_bias.reshape(group_n, own_bias)], axis=1
    )
    swapped = swap_blocks(side_grads.reshape(cube + (1, -1)), second[::-1]).reshape(group_n, -1)
    own_mods = swapped[:, : batches * own_ada].reshape(group_n * batches, own_ada)
    d_bias = jnp.sum(swapped[:, batches * own_ada :], axis=0)
    d_ada = jnp.einsum(
        "kr,kd->rd",
        own_mods,
        sc_all.reshape(group_n * batches, width_n).astype(jnp.float32),
        precision=lax.Precision.HIGHEST,
    )
    return (
        out.reshape(inputs.shape),
        d_x.reshape(inputs.shape),
        d_cond[:, None],
        d_ada[None],
        sums[0][None],
        sums[1][None],
        sums[2][None],
        d_bias[None],
    )


def solution(mesh):
    return jax.shard_map(
        local,
        mesh=mesh,
        in_specs=(
            P(None, "fsdp", None, None),
            P(None, "fsdp", None),
            P(None, "fsdp"),
            P(None, "fsdp", None),
            P(None, "fsdp", None),
            P(None, "fsdp", None),
            P(None, "fsdp", None),
            P(None, "fsdp"),
            P(None, "fsdp", None, None),
        ),
        out_specs=(
            P(None, "fsdp", None, None),
            P(None, "fsdp", None, None),
            P(None, "fsdp", None),
            P(None, "fsdp", None),
            P(None, "fsdp", None),
            P(None, "fsdp", None),
            P(None, "fsdp", None),
            P(None, "fsdp"),
        ),
        check_vma=False,
    )
```

```python
import functools
import math

import jax
import jax.numpy as jnp
from jax import lax
from jax.experimental import pallas as pl
from jax.experimental.pallas import tpu as pltpu
from jax.sharding import PartitionSpec as P

HEADS = 6

NORM_EPS = 1e-06


def product(form, left, right):
    return jnp.einsum(form, left, right, preferred_element_type=jnp.float32)


def dot_nn(left, right):
    return lax.dot_general(left, right, (((1,), (0,)), ((), ())), preferred_element_type=jnp.float32)


def dot_nt(left, right):
    return lax.dot_general(left, right, (((1,), (1,)), ((), ())), preferred_element_type=jnp.float32)


def dot_tn(left, right):
    return lax.dot_general(left, right, (((0,), (0,)), ((), ())), preferred_element_type=jnp.float32)


def layer_norm(values):
    center = values - jnp.mean(values, axis=-1, keepdims=True)
    inv_std = lax.rsqrt(jnp.mean(center * center, axis=-1, keepdims=True) + NORM_EPS)
    return (center * inv_std, inv_std)


def norm_back(grad_norm, normed, inv_std):
    return inv_std * (
        grad_norm
        - jnp.mean(grad_norm, axis=-1, keepdims=True)
        - normed * jnp.mean(grad_norm * normed, axis=-1, keepdims=True)
    )


def token_sum(values):
    return jnp.sum(values, axis=0, keepdims=True)


def pair_masks(rows, pair_w):
    lane = lax.broadcasted_iota(jnp.int32, (rows, pair_w), 1)
    return (lane < pair_w // 2, lane >= pair_w // 2)


def block_rows(me_ref, offset, block_n, bits=None):
    me = me_ref[0] if bits is None else me_ref[0] & bits
    return pl.ds(pl.multiple_of((me ^ offset) * block_n, 16), block_n)


def attend_kernel(
    batches, me_ref, x_ref, mod_ref, own_ref, other_ref, bias_ref,
    w_ref, h_ref, qkv_ref, p_ref, ctx_ref, ao_ref, mid_ref,
):
    block_n = own_ref.shape[1]
    for idx in range(own_ref.shape[0]):
        w_ref[block_rows(me_ref, 2 * idx, block_n, 1), :] = own_ref[idx]
        w_ref[block_rows(me_ref, 2 * idx + 1, block_n, 1), :] = other_ref[idx]
    tokens_n, width_n = x_ref.shape[0] // batches, x_ref.shape[1]
    pair_w = 2 * (width_n // HEADS)
    scaling = 1.0 / math.sqrt(width_n // HEADS)
    for b in range(batches):
        rows = pl.ds(b * tokens_n, tokens_n)
        normed, _ = layer_norm(x_ref[rows, :])
        shift = mod_ref[b, 0:1, :]
        scale = mod_ref[b, 1:2, :]
        h_ref[rows, :] = (normed * (1.0 + scale) + shift).astype(jnp.bfloat16)
    for part, bias_row in ((0, 6), (1, None), (2, 7)):
        cols = pl.ds(part * width_n, width_n)
        value = dot_nt(h_ref[...], w_ref[cols, :])
        if bias_row is not None:
            value = value + bias_ref[bias_row : bias_row + 1, :]
        qkv_ref[:, cols] = value.astype(jnp.bfloat16)
    masks = pair_masks(tokens_n, pair_w)
    for b in range(batches):
        rows = pl.ds(b * tokens_n, tokens_n)
        for pair in range(HEADS // 2):
            q_pair = qkv_ref[rows, pl.ds(pair * pair_w, pair_w)]
            k_pair = qkv_ref[rows, pl.ds(width_n + pair * pair_w, pair_w)]
            v_pair = qkv_ref[rows, pl.ds(2 * width_n + pair * pair_w, pair_w)]
            found = []
            for side in range(2):
                q_one = jnp.where(masks[side], q_pair, jnp.zeros_like(q_pair)) * jnp.bfloat16(scaling)
                scores = dot_nt(q_one, k_pair)
                expd = jnp.exp(scores - jnp.max(scores, axis=-1, keepdims=True))
                share = 1.0 / jnp.sum(expd, axis=-1, keepdims=True)
                probs = (expd * share).astype(jnp.bfloat16)
                p_ref[b * HEADS + 2 * pair + side] = probs
                found.append(dot_nn(probs, v_pair))
            ctx_ref[rows, pl.ds(pair * pair_w, pair_w)] = jnp.where(masks[0], *found).astype(jnp.bfloat16)
    attn_out = dot_nt(ctx_ref[...], w_ref[pl.ds(3 * width_n, width_n), :]) + bias_ref[8:9, :]
    ao_ref[...] = attn_out
    for b in range(batches):
        rows = pl.ds(b * tokens_n, tokens_n)
        mid_ref[rows, :] = x_ref[rows, :] + mod_ref[b, 2:3, :] * ao_ref[rows, :]


def mlp_kernel(
    batches, lists, me_ref, live_ref, mid_ref, grad_ref, mod_ref, bias_ref, b_in_ref,
    in_own_ref, in_other_ref, out_own_ref, out_other_ref,
    out_ref, dmid_ref, g0_ref, g1_ref, g2_ref, g3_ref, gb_in_ref, gb_out_ref, dmod_ref,
    h_ref, dmlp_ref, mlp_ref, dh_ref,
):
    step = pl.program_id(0)
    tokens_n, width_n = mid_ref.shape[0] // batches, mid_ref.shape[1]

    @pl.when(step == 0)
    def _():
        total = jnp.zeros((1, width_n), jnp.float32)
        for b in range(batches):
            rows = pl.ds(b * tokens_n, tokens_n)
            normed, _ = layer_norm(mid_ref[rows, :])
            h_ref[rows, :] = (normed * (1.0 + mod_ref[b, 4:5, :]) + mod_ref[b, 3:4, :]).astype(jnp.bfloat16)
            d_mlp = mod_ref[b, 5:6, :] * (live_ref[b].astype(jnp.float32) * grad_ref[rows, :])
            total = total + token_sum(d_mlp)
            dmlp_ref[rows, :] = d_mlp.astype(jnp.bfloat16)
        gb_out_ref[...] = total
        mlp_ref[...] = jnp.zeros_like(mlp_ref)
        dh_ref[...] = jnp.zeros_like(dh_ref)

    def piece(w_in_ref, w_out_ref, offsets, g_ref):
        blocks, both = g_ref.shape[0], g_ref.shape[1]
        one = both // 2
        w_in = jnp.concatenate([w_in_ref[(me_ref[0] ^ at) >> 1] for at in offsets], axis=0)
        w_out = jnp.concatenate([w_out_ref[(me_ref[0] ^ at) >> 1] for at in offsets], axis=0)
        pre = dot_nt(h_ref[...], w_in) + b_in_ref[...]
        root = math.sqrt(2.0 / math.pi)
        square = pre * pre
        tanh = jnp.tanh(root * (pre + 0.044715 * (square * pre)))
        half = 0.5 * (1.0 + tanh)
        act = (pre * half).astype(jnp.bfloat16)
        slope = half + (0.5 * pre) * (1.0 - tanh * tanh) * (root + (3.0 * 0.044715 * root) * square)
        d_pre = dot_nt(dmlp_ref[...], w_out) * slope
        mlp_ref[...] += dot_nn(act, w_out)
        g_ref[:, one:, :] = dot_tn(act, dmlp_ref[...]).astype(jnp.bfloat16).reshape(blocks, one, width_n)
        gb_in_ref[...] = token_sum(d_pre)
        d_pre_b = d_pre.astype(jnp.bfloat16)
        dh_ref[...] += dot_nn(d_pre_b, w_in)
        g_ref[:, :one, :] = dot_tn(d_pre_b, h_ref[...]).astype(jnp.bfloat16).reshape(blocks, one, width_n)

    other = (in_other_ref, out_other_ref)
    own = (in_own_ref, out_own_ref)
    for idx, args in enumerate(
        (
            (*other, lists[0], g0_ref),
            (*other, lists[1], g1_ref),
            (*own, lists[0], g2_ref),
            (*own, lists[1], g3_ref),
        )
    ):
        pl.when(step == idx)(functools.partial(piece, *args))

    @pl.when(step == pl.num_programs(0) - 1)
    def _():
        for b in range(batches):
            rows = pl.ds(b * tokens_n, tokens_n)
            live = live_ref[b].astype(jnp.float32)
            middle = mid_ref[rows, :]
            d_y = live * grad_ref[rows, :]
            mlp_out = mlp_ref[rows, :] + bias_ref[13:14, :]
            out_ref[rows, :] = live * (middle + mod_ref[b, 5:6, :] * mlp_out)
            normed, inv_std = layer_norm(middle)
            d_h = dh_ref[rows, :]
            dmod_ref[b, 0:1, :] = token_sum(d_h)
            dmod_ref[b, 1:2, :] = token_sum(d_h * normed)
            dmod_ref[b, 2:3, :] = token_sum(d_y * mlp_out)
            dmid_ref[rows, :] = d_y + norm_back(d_h * (1.0 + mod_ref[b, 4:5, :]), normed, inv_std)


def attend_back_kernel(
    batches, mod_ref, w_ref, qkv_ref, p_ref, ctx_ref, ao_ref, dmid_ref,
    dqkv_ref, g_ref, gb_ref, dgate_ref, dattn_ref, dctx_ref,
):
    tokens_n, width_n = dmid_ref.shape[0] // batches, dmid_ref.shape[1]
    pair_w = 2 * (width_n // HEADS)
    scaling = 1.0 / math.sqrt(width_n // HEADS)
    total = jnp.zeros((1, width_n), jnp.float32)
    for b in range(batches):
        rows = pl.ds(b * tokens_n, tokens_n)
        d_mid = dmid_ref[rows, :]
        dgate_ref[b, 0:1, :] = token_sum(d_mid * ao_ref[rows, :])
        d_attn = mod_ref[b, 2:3, :] * d_mid
        total = total + token_sum(d_attn)
        dattn_ref[rows, :] = d_attn.astype(jnp.bfloat16)
    gb_ref[2:3, :] = total
    dctx_ref[...] = dot_nn(dattn_ref[...], w_ref[pl.ds(3 * width_n, width_n), :]).astype(jnp.bfloat16)
    g_ref[...] = dot_tn(dattn_ref[...], ctx_ref[...]).astype(jnp.bfloat16)
    masks = pair_masks(tokens_n, pair_w)
    for pair in range(HEADS // 2):
        cols = pl.ds(pair * pair_w, pair_w)
        q_total = jnp.zeros((1, pair_w), jnp.float32)
        v_total = jnp.zeros((1, pair_w), jnp.float32)
        for b in range(batches):
            rows = pl.ds(b * tokens_n, tokens_n)
            q_pair = qkv_ref[rows, cols]
            k_pair = qkv_ref[rows, pl.ds(width_n + pair * pair_w, pair_w)]
            v_pair = qkv_ref[rows, pl.ds(2 * width_n + pair * pair_w, pair_w)]
            dc_pair = dctx_ref[rows, cols]
            d_q, d_k, d_v = [], [], []
            for side in range(2):
                probs_b = p_ref[b * HEADS + 2 * pair + side]
                probs = probs_b.astype(jnp.float32)
                dc_one = jnp.where(masks[side], dc_pair, jnp.zeros_like(dc_pair))
                d_probs = dot_nt(dc_one, v_pair)
                row_dot = jnp.sum(probs * d_probs, axis=-1, keepdims=True)
                d_scores = (probs * (d_probs - row_dot)).astype(jnp.bfloat16)
                d_v.append(dot_tn(probs_b, dc_pair))
                d_q.append(dot_nn(d_scores, k_pair))
                d_k.append(dot_tn(d_scores, q_pair))
            d_query = jnp.where(masks[0], *d_q) * scaling
            d_key = jnp.where(masks[0], *d_k) * scaling
            d_value = jnp.where(masks[0], *d_v)
            q_total = q_total + token_sum(d_query)
            v_total = v_total + token_sum(d_value)
            dqkv_ref[rows, cols] = d_query.astype(jnp.bfloat16)
            dqkv_ref[rows, pl.ds(width_n + pair * pair_w, pair_w)] = d_key.astype(jnp.bfloat16)
            dqkv_ref[rows, pl.ds(2 * width_n + pair * pair_w, pair_w)] = d_value.astype(jnp.bfloat16)
        gb_ref[0:1, cols] = q_total
        gb_ref[1:2, cols] = v_total
def project_back_kernel(
    batches, offsets, me_ref, x_ref, mod_ref, w_ref, h_ref, dqkv_ref, g_out_ref, dmid_ref,
    dx_ref, keep_ref, send_ref, dmod_ref, g_ref,
):
    tokens_n, width_n = x_ref.shape[0] // batches, x_ref.shape[1]
    for part in range(3):
        cols = pl.ds(part * width_n, width_n)
        g_ref[cols, :] = dot_tn(dqkv_ref[:, cols], h_ref[...]).astype(jnp.bfloat16)
    g_ref[pl.ds(3 * width_n, width_n), :] = g_out_ref[...]
    half, block_n = keep_ref.shape[0], keep_ref.shape[1]
    for idx, offset in enumerate(offsets):
        target = keep_ref if idx < half else send_ref
        target[idx % half] = g_ref[block_rows(me_ref, offset, block_n), :]
    d_h_all = dot_nn(dqkv_ref[...], w_ref[pl.ds(0, 3 * width_n), :])
    for b in range(batches):
        rows = pl.ds(b * tokens_n, tokens_n)
        normed, inv_std = layer_norm(x_ref[rows, :])
        d_h = d_h_all[b * tokens_n : (b + 1) * tokens_n]
        dmod_ref[b, 0:1, :] = token_sum(d_h)
        dmod_ref[b, 1:2, :] = token_sum(d_h * normed)
        dx_ref[rows, :] = dmid_ref[rows, :] + norm_back(d_h * (1.0 + mod_ref[b, 1:2, :]), normed, inv_std)


def shaped(shape, dtype):
    return jax.ShapeDtypeStruct(shape, dtype)


SCALARS = pl.BlockSpec(memory_space=pltpu.SMEM)


def blocks_in(count):
    return [pl.BlockSpec(memory_space=pltpu.VMEM)] * count


def cost(flops, moved, exps=0):
    return pl.CostEstimate(flops=flops, bytes_accessed=moved, transcendentals=exps)


def attend(me, x_rows, mods, own, other, bias_rows):
    batches = mods.shape[0]
    total_n, width_n = x_rows.shape
    tokens_n = total_n // batches
    return pl.pallas_call(
        functools.partial(attend_kernel, batches),
        in_specs=[SCALARS] + blocks_in(5),
        out_shape=(
            shaped((4 * width_n, width_n), jnp.bfloat16),
            shaped((total_n, width_n), jnp.bfloat16),
            shaped((total_n, 3 * width_n), jnp.bfloat16),
            shaped((batches * HEADS, tokens_n, tokens_n), jnp.bfloat16),
            shaped((total_n, width_n), jnp.bfloat16),
            shaped((total_n, width_n), jnp.float32),
            shaped((total_n, width_n), jnp.float32),
        ),
        cost_estimate=cost(8 * total_n * width_n * (width_n + tokens_n), 9 << 20, 800000),
        name="attend",
    )(me, x_rows, mods, own, other, bias_rows)


def mlp(me, live_flags, middle, grad_rows, mods, bias_rows, bias_in, weights, lists, piece_shape):
    batches = mods.shape[0]
    total_n, width_n = middle.shape
    hidden = bias_in.shape[1]
    whole = lambda *shape: pl.BlockSpec(shape, lambda i: (0,) * len(shape))
    line = pl.BlockSpec((1, hidden // 4), lambda i: (0, i))
    return pl.pallas_call(
        functools.partial(mlp_kernel, batches, lists),
        grid=(4,),
        in_specs=[
            SCALARS,
            SCALARS,
            whole(total_n, width_n),
            whole(total_n, width_n),
            whole(*mods.shape),
            whole(*bias_rows.shape),
            line,
        ]
        + [whole(*value.shape) for value in weights],
        out_specs=[whole(total_n, width_n)] * 2
        + [whole(*piece_shape)] * 4
        + [line, whole(1, width_n), whole(batches, 3, width_n)],
        out_shape=[shaped((total_n, width_n), jnp.float32)] * 2
        + [shaped(piece_shape, jnp.bfloat16)] * 4
        + [
            shaped((1, hidden), jnp.float32),
            shaped((1, width_n), jnp.float32),
            shaped((batches, 3, width_n), jnp.float32),
        ],
        scratch_shapes=[
            pltpu.VMEM((total_n, width_n), jnp.bfloat16),
            pltpu.VMEM((total_n, width_n), jnp.bfloat16),
            pltpu.VMEM((total_n, width_n), jnp.float32),
            pltpu.VMEM((total_n, width_n), jnp.float32),
        ],
        cost_estimate=cost(12 * total_n * width_n * hidden, 9 << 20, total_n * hidden),
        name="mlp",
    )(me, live_flags, middle, grad_rows, mods, bias_rows, bias_in, *weights)


def attend_back(mods, weight, qkv, probs, context, attn_out, d_mid):
    batches = mods.shape[0]
    total_n, width_n = d_mid.shape
    return pl.pallas_call(
        functools.partial(attend_back_kernel, batches),
        out_shape=(
            shaped((total_n, 3 * width_n), jnp.bfloat16),
            shaped((width_n, width_n), jnp.bfloat16),
            shaped((3, width_n), jnp.float32),
            shaped((batches, 1, width_n), jnp.float32),
        ),
        scratch_shapes=[
            pltpu.VMEM((total_n, width_n), jnp.bfloat16),
            pltpu.VMEM((total_n, width_n), jnp.bfloat16),
        ],
        cost_estimate=cost(8 * total_n * width_n * width_n, 9 << 20),
        name="attend_back",
    )(mods, weight, qkv, probs, context, attn_out, d_mid)


def project_back(me, x_rows, mods, weight, h_in, d_qkv, g_out, d_mid, offsets, block_shape):
    batches = mods.shape[0]
    total_n, width_n = x_rows.shape
    return pl.pallas_call(
        functools.partial(project_back_kernel, batches, offsets),
        in_specs=[SCALARS] + blocks_in(7),
        out_shape=(
            shaped((total_n, width_n), jnp.float32),
            shaped(block_shape, jnp.bfloat16),
            shaped(block_shape, jnp.bfloat16),
            shaped((batches, 2, width_n), jnp.float32),
        ),
        scratch_shapes=[pltpu.VMEM((4 * width_n, width_n), jnp.bfloat16)],
        cost_estimate=cost(12 * total_n * width_n * width_n, 8 << 20),
        name="project_back",
    )(me, x_rows, mods, weight, h_in, d_qkv, g_out, d_mid)


def exchange(value, bit_idx):
    group_n = lax.axis_size("fsdp")
    return lax.ppermute(value, "fsdp", [(dev, dev ^ (1 << bit_idx)) for dev in range(group_n)])


def offsets_of(order):
    return [
        sum(((q >> at) & 1) << bit_idx for at, bit_idx in enumerate(order))
        for q in range(1 << len(order))
    ]


def together(*values):
    return lax.optimization_barrier(values)


def gather_blocks(blocks, order):
    for bit_idx in order:
        blocks = jnp.concatenate([blocks, exchange(blocks, bit_idx)], axis=0)
    return blocks


def gather_ordered(block, order):
    high = max(order)
    cur = block.reshape((1,) * high + block.shape)
    for bit_idx in order:
        other = exchange(cur, bit_idx)
        upper = (lax.axis_index("fsdp") >> bit_idx) & 1 == 1
        cur = jnp.concatenate(
            [jnp.where(upper, other, cur), jnp.where(upper, cur, other)], axis=high - bit_idx
        )
    return cur.reshape((-1,) + block.shape)


def add(left, right, dtype=jnp.bfloat16):
    return (left.astype(jnp.float32) + right.astype(jnp.float32)).astype(dtype)


def scatter_step(keep, other, bit_idx):
    half = keep.shape[0] // 2
    upper = exchange(add(keep[half:], other[half:], keep.dtype), bit_idx)
    return add(keep[:half], other[:half], keep.dtype), upper


def local(inputs, cond, live, ada_w, attn_w, fc1_w, fc2_w, biases, grad_out):
    group_n = lax.axis_size("fsdp")
    count = group_n.bit_length() - 1
    far, near = list(range(count - 1, 2, -1)), [1, 2]
    me = lax.axis_index("fsdp").astype(jnp.int32)
    me_line = me.reshape(1)
    width_n = attn_w.shape[2]
    batches = inputs.shape[0]
    own_attn, own_ada, own_bias = attn_w.shape[1], ada_w.shape[1], biases.shape[1]
    own_hidden = fc1_w.shape[1]

    def chosen(offsets):
        sources = me ^ jnp.array(offsets, jnp.int32)
        return (sources[:, None] == jnp.arange(group_n, dtype=jnp.int32)[None]).astype(jnp.float32)

    def pick(form, left, right):
        return jnp.einsum(form, left, right, precision=lax.Precision.HIGHEST)

    cond_rows = cond[:, 0]
    sigmoid_c = jax.nn.sigmoid(cond_rows)
    sc_own = (cond_rows * sigmoid_c).astype(jnp.bfloat16)
    bias_line = jnp.pad(biases, ((0, 0), (0, width_n - own_bias)))
    pad_rows = -(own_ada + 1 + batches) % 16
    attn_order = far + near + [0]
    attn_offsets = offsets_of(attn_order)
    attn_pick = chosen(attn_offsets)
    ada_own = jnp.concatenate(
        [ada_w[0], bias_line, sc_own, jnp.zeros((pad_rows, width_n), jnp.bfloat16)], axis=0
    )[None]
    attn_own = gather_ordered(attn_w[0], far + near[::-1])
    ada_own = gather_ordered(ada_own[0], far + near)
    in_own = gather_ordered(fc1_w[0], far + near[::-1])
    out_own = gather_ordered(fc2_w[0], far + near)
    attn_other = exchange(attn_own, 0)
    ada_other = exchange(ada_own, 0)
    weights = [in_own, exchange(in_own, 0), out_own, exchange(out_own, 0)]
    ada_halves = (ada_own, ada_other)
    odd = me & 1 == 1

    def interleaved(own, other, axis):
        return jnp.stack([jnp.where(odd, other, own), jnp.where(odd, own, other)], axis=axis + 1).reshape(
            own.shape[:axis] + (group_n,) + own.shape[axis + 1 :]
        )

    side_all = interleaved(*[part[:, own_ada : own_ada + 1 + batches] for part in ada_halves], 0)
    bias_rows = side_all[:, 0, :own_bias].astype(jnp.float32).reshape(-1, width_n)
    mod_blocks = interleaved(
        *[
            product("bd,ed->be", sc_own, part.reshape(-1, width_n)).reshape(
                batches, group_n // 2, -1
            )
            for part in ada_halves
        ],
        1,
    )
    mods = mod_blocks[:, :, :own_ada].reshape(batches, 6, width_n) + bias_rows[:6]
    block_shape = attn_own.shape
    even = own_attn % 16 == 0
    if not even:
        table = me ^ jnp.array(attn_offsets, jnp.int32)
        ordered = interleaved(attn_own, attn_other, 0)
        halves = ordered.reshape(2, 1, 2 * width_n, width_n)
        attn_in = (halves[0], halves[1])
    else:
        attn_in = (attn_own, attn_other)
    a_offsets = offsets_of(far[:-1] + near[::-1])
    b_offsets = [one ^ (1 << far[-1]) for one in offsets_of(far[:-1] + near)]
    hidden_offsets = (
        [one ^ 1 for one in a_offsets] + [one ^ 1 for one in b_offsets] + a_offsets + b_offsets
    )
    hidden_pick = chosen(hidden_offsets)
    bias_in = pick(
        "qj,je->qe", hidden_pick, bias_rows[9:-1].reshape(group_n, own_hidden)
    ).reshape(1, -1)

    lists = [a_offsets, b_offsets]
    piece_shape = (group_n // 4, 2 * own_hidden, width_n)

    def unpacked(piece):
        parts = piece.reshape(2, -1, own_hidden, width_n).swapaxes(0, 1)
        return parts.reshape(-1, 2 * own_hidden, width_n)

    x_rows = inputs.reshape(-1, width_n)
    plain = [0, 1]
    weight, h_in, qkv, probs, context, attn_out, middle = attend(
        me_line if even else jnp.zeros_like(me_line),
        x_rows,
        mods,
        attn_in[0],
        attn_in[1],
        bias_rows,
    )
    if own_hidden % 16:
        own_table = (me ^ jnp.array(a_offsets + b_offsets, jnp.int32)) >> 1
        weights = [value[own_table].reshape(2, -1, width_n) for value in weights]
        lists = [[0], [2]]
        piece_shape = (1, group_n // 4 * 2 * own_hidden, width_n)
    out, d_mid, g_a_send, g_b_send, g_a, g_b, gb_in, gb_out, dmod_b = mlp(
        jnp.zeros_like(me_line) if own_hidden % 16 else me_line,
        live[:, 0],
        middle,
        grad_out.reshape(-1, width_n),
        mods,
        bias_rows,
        bias_in,
        weights,
        lists,
        piece_shape,
    )
    g_hidden = [g_a_send, g_b_send, g_a, g_b]
    if own_hidden % 16:
        g_hidden = [unpacked(piece) for piece in g_hidden]
    g_a_send, g_b_send, g_a, g_b = g_hidden
    got_a, got_b = exchange(g_a_send, 0), exchange(g_b_send, 0)
    d_qkv, g_out, gb_attn, d_gate = attend_back(
        mods, weight, qkv, probs, context, attn_out, d_mid
    )
    got_a, got_b, d_qkv, g_out = together(got_a, got_b, d_qkv, g_out)
    g_a, got_a = scatter_step(g_a, got_a, near[0])
    g_b, got_b = scatter_step(g_b, got_b, near[1])
    d_x, g_keep, g_send, dmod_a = project_back(
        me_line if even else jnp.zeros_like(me_line),
        x_rows,
        mods,
        weight,
        h_in,
        d_qkv,
        g_out,
        d_mid,
        attn_offsets if even else plain,
        block_shape if even else (1, 2 * width_n, width_n),
    )
    if not even:
        ordered = jnp.concatenate([g_keep, g_send], axis=1).reshape((group_n,) + block_shape[1:])[table]
        g_keep, g_send = ordered[: group_n // 2], ordered[group_n // 2 :]
    got_a, got_b, g_send, dmod_a = together(got_a, got_b, g_send, dmod_a)
    top = count - 1
    g_attn, got = g_keep, exchange(g_send, 0)
    g_a, got_a = scatter_step(g_a, got_a, near[1])
    g_b, got_b = scatter_step(g_b, got_b, near[0])
    d_mods = jnp.concatenate([dmod_a, d_gate, dmod_b], axis=1)
    true_in = pick("qj,qe->je", hidden_pick, gb_in.reshape(group_n, own_hidden))
    g_bias = jnp.concatenate(
        [jnp.sum(d_mods, axis=0), gb_attn, true_in.reshape(-1, width_n), gb_out], axis=0
    )
    mod_blocks = d_mods.reshape(batches, group_n, own_ada)
    side_n = batches * own_ada + own_bias
    row_n = -(-side_n // width_n)
    side_blocks = jnp.concatenate(
        [mod_blocks[idx] for idx in range(batches)]
        + [
            g_bias.reshape(group_n, own_bias),
            jnp.zeros((group_n, row_n * width_n - side_n), jnp.float32),
        ],
        axis=1,
    )
    side_blocks = pick("qj,je->qe", attn_pick, side_blocks)
    side_blocks = side_blocks.astype(jnp.bfloat16).reshape(group_n, row_n, width_n)

    def send(values, blocks, at):
        split = blocks.reshape((-1, 2, 1 << at) + blocks.shape[1:])
        parts = [*values, split[:, 1:]]
        flat = [part.reshape(-1, width_n) for part in parts]
        both = exchange(jnp.concatenate(flat, axis=0), attn_order[at]) if values else exchange(flat[0], attn_order[at])
        came, start = [], 0
        for part, rows in zip(parts, flat):
            came.append(both[start : start + rows.shape[0]].reshape(part.shape))
            start += rows.shape[0]
        return came[:-1], jnp.concatenate([split[:, :1], came[-1]], axis=1).reshape(blocks.shape)

    def halves(keep, other):
        half = keep.shape[0] // 2
        return add(keep[:half], other[:half]), add(keep[half:], other[half:])

    _, side_blocks = send([], side_blocks, top)
    got, got_a, got_b, side_blocks = together(got, got_a, got_b, side_blocks)
    for at in range(top - 1, len(far) - 1, -1):
        g_attn, upper = halves(g_attn, got)
        (got,), side_blocks = send([upper], side_blocks, at)
    g_hid, upper_hid = add(g_a, got_a), add(g_b, got_b)
    for at in range(len(far) - 1, -1, -1):
        g_attn, upper = halves(g_attn, got)
        if at < len(far) - 1:
            g_hid, upper_hid = halves(g_hid, got_hid)
        (got, got_hid), side_blocks = send([upper, upper_hid], side_blocks, at)
    mod_pairs = mod_blocks.reshape(batches, group_n // 2, 2, own_ada)
    d_sc = sum(
        jnp.einsum(
            "bqr,qrd->bd",
            jnp.pad(
                lax.dynamic_index_in_dim(mod_pairs, (me & 1) ^ side, 2, keepdims=False),
                ((0, 0), (0, 0), (0, part.shape[1] - own_ada)),
            ),
            part.astype(jnp.float32),
            precision=lax.Precision.HIGHEST,
        )
        for side, part in enumerate(ada_halves)
    )
    d_cond = d_sc * sigmoid_c * (1.0 + cond_rows * (1.0 - sigmoid_c))
    side_got = side_blocks.reshape(group_n, -1).astype(jnp.float32)
    own_mods = side_got[:, : batches * own_ada].reshape(group_n, batches, own_ada)
    d_bias = jnp.sum(side_got[:, batches * own_ada : side_n], axis=0)
    sc_all = pick("qj,jbd->qbd", attn_pick, side_all[:, 1:].astype(jnp.float32))
    d_ada = pick("qbr,qbd->rd", own_mods, sc_all)
    d_attn = add(g_attn, got, jnp.float32)
    d_hidden = add(g_hid, got_hid, jnp.float32)
    return (
        out.reshape(inputs.shape),
        d_x.reshape(inputs.shape),
        d_cond[:, None],
        d_ada[None],
        d_attn,
        d_hidden[:, :own_hidden],
        d_hidden[:, own_hidden:],
        d_bias[None],
    )


def solution(mesh):
    return jax.shard_map(
        local,
        mesh=mesh,
        in_specs=(
            P(None, "fsdp", None, None),
            P(None, "fsdp", None),
            P(None, "fsdp"),
            P(None, "fsdp", None),
            P(None, "fsdp", None),
            P(None, "fsdp", None),
            P(None, "fsdp", None),
            P(None, "fsdp"),
            P(None, "fsdp", None, None),
        ),
        out_specs=(
            P(None, "fsdp", None, None),
            P(None, "fsdp", None, None),
            P(None, "fsdp", None),
            P(None, "fsdp", None),
            P(None, "fsdp", None),
            P(None, "fsdp", None),
            P(None, "fsdp", None),
            P(None, "fsdp"),
        ),
        check_vma=False,
    )
```
